512 devices in a mesh: chan: 16 (over z), inp: 32 (over x, y, core).
Axes of the slice: x: 4, y: 4, z: 16, core: 2. Of those that a mesh axis runs over, the one named last changes fastest.
Arguments:
- voltages: int32 [2, 1024, 16, 4096], P(None, 'chan', None, 'inp'), may hold values from -128 to 127
- fir_taps: float32 [4, 16], replicated, may hold values from -3 to 3
Outputs:
- visibilities: float32 [16, 2, 4096, 4096], P('chan', None, 'inp')
The draws below stay inside these ranges and needn't reach their ends.
All inputs are finite; a program needn't handle non-finite values.
Results may differ from the reference program's by a relative error of at most 0.0036.
Values may be sent and summed in bfloat16 or wider, within the bound.
A program may use at most 128 MiB of HBM per device.

```python
import math
import jax
import jax.numpy as jnp
from jax import lax

INPUTS = 4096
CH = 16
TAPS = 4
SPECTRA = 1024


def plant(array, own_key, smallest, high):
    longest = array.shape.index(max(array.shape))
    spots = []
    for shift in (0, 1):
        where = [jax.random.randint(jax.random.fold_in(own_key, axis), (), 0, length) for axis, length in enumerate(array.shape)]
        where[longest] = (where[longest] + shift) % array.shape[longest]
        spots.append(tuple(where))
    return array.at[spots[0]].set(smallest).at[spots[1]].set(high)


def noise(stream_key, extent, deviation, limit, kind=jnp.bfloat16):
    return jnp.clip(deviation * jax.random.normal(stream_key, extent, jnp.float32), -limit, limit).astype(kind)


def setup_inputs(seed: int = 0) -> dict:
    key_list = jax.random.split(jax.random.key(seed), 3)
    voltages = plant(jax.random.randint(key_list[0], (2, SPECTRA, CH, INPUTS), -128, 128), jax.random.fold_in(key_list[0], 1), -128, 127).astype(jnp.int32)
    fir_taps = noise(key_list[1], (TAPS, CH), 0.5, 3.0, jnp.float32)
    return dict(voltages=voltages, fir_taps=fir_taps)


volt_scale = 1.0 / 256.0


def dft_tables(count):
    index = jnp.arange(count, dtype=jnp.int32)
    phase = (index[:, None] * index[None, :]) % count
    angle = phase.astype(jnp.float32) * (2.0 * math.pi / count)
    return jnp.cos(angle), jnp.sin(angle)


def transform(filtered, count):
    cosine, sine = dft_tables(count)
    real_in = filtered[0]
    imag_in = filtered[1]
    high = lax.Precision.HIGHEST
    real_out = jnp.einsum("cn,snb->csb", cosine, real_in, precision=high) + jnp.einsum("cn,snb->csb", sine, imag_in, precision=high)
    imag_out = jnp.einsum("cn,snb->csb", cosine, imag_in, precision=high) - jnp.einsum("cn,snb->csb", sine, real_in, precision=high)
    return (jnp.stack([real_out, imag_out], 1) * volt_scale).astype(jnp.bfloat16)


def reference(voltages, fir_taps):
    volts = voltages.astype(jnp.float32)
    padded = jnp.concatenate([jnp.zeros((2, TAPS - 1, CH, INPUTS), jnp.float32), volts], 1)
    filtered = fir_taps[0][None, None, :, None] * padded[:, TAPS - 1:TAPS - 1 + SPECTRA]
    for tap_index in range(1, TAPS):
        begin = TAPS - 1 - tap_index
        filtered = filtered + fir_taps[tap_index][None, None, :, None] * padded[:, begin:begin + SPECTRA]
    channelized = transform(filtered, CH)
    norm_factor = 1.0 / SPECTRA

    def one_channel(panel):
        values = panel.astype(jnp.float32)
        rotated = jnp.stack([-values[1], values[0]], 0)
        real_part = jnp.einsum("psi,psj->ij", values, values)
        imag_part = jnp.einsum("psi,psj->ij", values, rotated)
        return jnp.stack([real_part, imag_part], 0) * norm_factor

    return lax.map(one_channel, channelized)
```

```python
import functools
import math

import jax
import jax.numpy as jnp
from jax import lax
from jax.experimental import pallas as pl
from jax.experimental.pallas import tpu as pltpu
from jax.sharding import PartitionSpec as P

volt_scale = 1.0 / 256.0


def passed_along(x, axis, by):
    count = lax.axis_size(axis)
    pairs = [(i, i + by) for i in range(count) if 0 <= i + by < count]
    return lax.ppermute(x, axis, pairs)


def dft_tables(count):
    index = jnp.arange(count, dtype=jnp.int32)
    phase = index[:, None] * index[None, :] % count
    angle = phase.astype(jnp.float32) * (2.0 * math.pi / count)
    return (jnp.cos(angle), jnp.sin(angle))


def transform(filtered, count):
    cosine, sine = dft_tables(count)
    real_in = filtered[0]
    imag_in = filtered[1]
    high = lax.Precision.HIGHEST
    real_out = jnp.einsum("cn,snb->csb", cosine, real_in, precision=high) + jnp.einsum(
        "cn,snb->csb", sine, imag_in, precision=high
    )
    imag_out = jnp.einsum("cn,snb->csb", cosine, imag_in, precision=high) - jnp.einsum(
        "cn,snb->csb", sine, real_in, precision=high
    )
    return (jnp.stack([real_out, imag_out], 1) * volt_scale).astype(jnp.bfloat16)


grid_x = 4
grid_y = 4
MESH = pl.DeviceIdType.MESH


def exchange_kernel(
    zs, spectra, out, store,
    sem_a, sem_b, sem_c, sem_d, sem_d2, sem_e, sem_e2, sem_p, send_a, send_g, send_p,
):
    rounds = zs // 2
    chips = grid_x * grid_y
    span = spectra.shape[2]
    lanes = spectra.shape[3]
    z = lax.axis_index("chan")
    inp = lax.axis_index("inp")
    core = lax.rem(inp, 2)
    chip = lax.div(inp, 2)
    y = lax.rem(chip, grid_y)
    x = lax.div(chip, grid_y)

    def chip_of(part, u, v):
        first, second = (u, v) if part == 0 else (v, u)
        return lax.rem(first + 4, 4) * grid_y + lax.rem(second + 4, 4)

    here = ((x, y), (y, x))
    barrier = pltpu.get_barrier_semaphore()

    def greet_z(step, carry):
        pl.semaphore_signal(
            barrier, inc=1, device_id={"chan": lax.rem(z + step, zs)}, device_id_type=MESH
        )
        return carry

    lax.fori_loop(1, zs, greet_z, 0)
    for du, dv in ((1, 0), (-1, 0), (0, 1), (0, -1)):
        pl.semaphore_signal(
            barrier, inc=1,
            device_id={"inp": chip_of(0, x + du, y + dv) * 2 + core}, device_id_type=MESH,
        )
    pl.semaphore_signal(barrier, inc=1, device_id={"inp": chip * 2 + 1 - core}, device_id_type=MESH)

    out[...] = jnp.zeros_like(out)
    pl.semaphore_wait(barrier, zs + 4)

    def z_slot(source):
        rows = pl.ds(pl.multiple_of(lax.rem(source, 2) * span, span), span)
        return store.at[lax.div(source, 2), core, :, chip, rows]

    own_copy = pltpu.make_async_copy(spectra.at[z], z_slot(z), sem_a.at[z])
    own_copy.start()

    def turn(step, carry):
        away = lax.div(step, 2) + 1
        target = lax.rem(z + (1 - 2 * lax.rem(step, 2)) * away + zs, zs)
        pltpu.make_async_remote_copy(
            src_ref=spectra.at[target], dst_ref=z_slot(z), send_sem=send_a, recv_sem=sem_a.at[z],
            device_id={"chan": target}, device_id_type=MESH,
        ).start()
        return carry

    lax.fori_loop(0, zs - 1, turn, 0)

    def pair_of(turn_index):
        off = lax.div(turn_index + 1, 2) * (2 * lax.rem(turn_index, 2) - 1)
        return lax.rem(lax.div(z, 2) + off + rounds, rounds)

    def arrive(sem, ref):
        pltpu.make_async_copy(ref, ref, sem).wait()

    def pass_on(t, pair, part, source, target, sem):
        block = store.at[pair, core, part, source]
        pltpu.make_async_remote_copy(
            src_ref=block, dst_ref=block, send_sem=send_g.at[t], recv_sem=sem.at[t],
            device_id={"inp": target * 2 + core}, device_id_type=MESH,
        ).start()

    def stage(t, action):
        @pl.when(jnp.logical_and(t >= 0, t < rounds))
        def _():
            action(t, pair_of(t))

    def step_a(t, pair):
        for source in (2 * pair, 2 * pair + 1):
            arrive(sem_a.at[source], z_slot(source))
        for part in (0, 1):
            u, v = here[part]
            for way in (1, -1):
                pass_on(t, pair, part, chip, chip_of(part, u + way, v), sem_b)

    def step_b(t, pair):
        arrive(sem_b.at[t], store.at[pair, core, :, pl.ds(0, 2)])
        for part in (0, 1):
            u, v = here[part]
            way = 1 - 2 * lax.rem(t + part, 2)
            pass_on(t, pair, part, chip_of(part, u - way, v), chip_of(part, u + way, v), sem_c)
        for shift in (0, 1, -1):
            for part in (0, 1):
                u, v = here[part]
                for way in (1, -1):
                    pass_on(t, pair, part, chip_of(part, u + shift, v), chip_of(part, u, v + way), sem_d)

    def step_c(t, pair):
        arrive(sem_c.at[t], store.at[pair, core, :, 0])
        for part in (0, 1):
            u, v = here[part]
            for way in (1, -1):
                pass_on(t, pair, part, chip_of(part, u + 2, v), chip_of(part, u, v + way), sem_d2)

    def across(t, pair, shift, sem):
        for part in (0, 1):
            u, v = here[part]
            way = 1 - 2 * lax.rem(t + part + u + shift + 4, 2)
            pass_on(t, pair, part, chip_of(part, u + shift, v - way), chip_of(part, u, v + way), sem)

    def step_d(t, pair):
        arrive(sem_d.at[t], store.at[pair, core, :, pl.ds(0, 6)])
        for shift in (0, 1, -1):
            across(t, pair, shift, sem_e)

    def step_d2(t, pair):
        arrive(sem_d2.at[t], store.at[pair, core, :, pl.ds(0, 2)])
        across(t, pair, 2, sem_e2)

    def step_e(t, pair):
        arrive(sem_e.at[t], store.at[pair, core, :, pl.ds(0, 3)])
        arrive(sem_e2.at[t], store.at[pair, core, :, 0])
        block = store.at[pair, core]
        pltpu.make_async_remote_copy(
            src_ref=block, dst_ref=block, send_sem=send_p.at[t], recv_sem=sem_p.at[t],
            device_id={"inp": chip * 2 + 1 - core}, device_id_type=MESH,
        ).start()

    def correlate(t, pair):
        arrive(sem_p.at[t], store.at[pair, 1 - core])
        real = store[pair, core, 0, chip].astype(jnp.float32).T
        imag = store[pair, core, 1, chip].astype(jnp.float32).T
        rows = jnp.concatenate(
            [jnp.concatenate([real, imag], 1), jnp.concatenate([imag, -real], 1)], 0
        ).astype(jnp.bfloat16)

        def one_chip(n, carry):
            block = jnp.concatenate(
                [
                    jnp.concatenate([store[pair, 0, part, n], store[pair, 1, part, n]], 1)
                    for part in (0, 1)
                ],
                0,
            )
            product = jnp.dot(rows, block, preferred_element_type=jnp.float32)
            columns = pl.ds(pl.multiple_of(n * (2 * lanes), 2 * lanes), 2 * lanes)
            out[0, 0, :, columns] += product[:lanes]
            out[0, 1, :, columns] += product[lanes:]
            return carry

        lax.fori_loop(0, chips, one_chip, 0)

    def iteration(it, carry):
        stage(it, step_a)
        stage(it - 1, step_b)
        stage(it - 2, step_c)
        stage(it - 2, step_d)
        stage(it - 3, step_d2)
        stage(it - 4, step_e)
        stage(it - 5, correlate)
        return carry

    lax.fori_loop(0, rounds + 5, iteration, 0)

    arrive(send_a, spectra.at[pl.ds(0, zs - 1)])

    def drain(t, carry):
        arrive(send_g.at[t], store.at[0, 0, :, pl.ds(0, 15)])
        arrive(send_p.at[t], store.at[0, 0])
        return carry

    lax.fori_loop(0, rounds, drain, 0)


def exchange(spectra):
    zs, parts, span, lanes = spectra.shape
    rounds = zs // 2
    chips = grid_x * grid_y
    dma = pltpu.SemaphoreType.DMA
    return pl.pallas_call(
        functools.partial(exchange_kernel, zs),
        out_shape=jax.ShapeDtypeStruct((1, 2, lanes, 2 * chips * lanes), jnp.float32),
        in_specs=[pl.BlockSpec(memory_space=pltpu.VMEM)],
        out_specs=pl.BlockSpec(memory_space=pltpu.VMEM),
        scratch_shapes=[pltpu.VMEM((rounds, 2, 2, chips, 2 * span, lanes), jnp.bfloat16), dma((zs,))]
        + [dma((rounds,))] * 7
        + [dma, dma((rounds,)), dma((rounds,))],
        compiler_params=pltpu.CompilerParams(
            collective_id=0, has_side_effects=True, vmem_limit_bytes=40 * 1024 * 1024
        ),
    )(spectra)


def body(voltages, fir_taps):
    frames = voltages.shape[1]
    chans = voltages.shape[2]
    tap_count = fir_taps.shape[0]
    early_rim = passed_along(voltages[:, frames - (tap_count - 1) :], "chan", 1)
    extended = jnp.concatenate([early_rim, voltages], 1).astype(jnp.float32)
    filtered = (
        fir_taps[0][None, None, :, None] * extended[:, tap_count - 1 : tap_count - 1 + frames]
    )
    for tap_index in range(1, tap_count):
        begin = tap_count - 1 - tap_index
        filtered = (
            filtered
            + fir_taps[tap_index][None, None, :, None] * extended[:, begin : begin + frames]
        )
    spectra = transform(filtered, chans)
    norm_factor = 1.0 / (frames * lax.axis_size("chan"))
    return exchange(spectra) * norm_factor


def solution(mesh):
    placed = (P(None, "chan", None, "inp"), P())
    return jax.shard_map(
        body, mesh=mesh, in_specs=placed, out_specs=P("chan", None, "inp", None), check_vma=False
    )
```

```python
import functools
import math

import jax
import jax.numpy as jnp
import numpy as np
from jax import lax
from jax.experimental import pallas as pl
from jax.experimental.pallas import tpu as pltpu
from jax.sharding import PartitionSpec as P


def passed_along(x, axis, by):
    count = lax.axis_size(axis)
    pairs = [(i, i + by) for i in range(count) if 0 <= i + by < count]
    return lax.ppermute(x, axis, pairs)


def dft_rows(count, tap_count):
    index = np.arange(count)
    angle = (index[:, None] * index[None, :] % count) * (2.0 * math.pi / count)
    cosine, sine = np.cos(angle), np.sin(angle)
    real_out = np.concatenate([cosine, sine], 1)
    imag_out = np.concatenate([-sine, cosine], 1)
    rows = np.stack([real_out, imag_out], 1).reshape(2 * count, 2 * count)
    return np.tile(rows, (1, tap_count)).astype(np.float32)


volt_scale = 1.0 / 256.0
LAGS = (2, 4, 6, 6, 8, 12)
grid_x = 4
grid_y = 4
MESH = pl.DeviceIdType.MESH


def exchange_kernel(
    zs, volts, rim, taps, table, out, store, rows, frames, stage_f32, spectra,
    sem_a, sem_b, sem_c, sem_d, sem_f, sem_g, sem_p, send_a, send_b, send_r, send_p,
):
    chips = grid_x * grid_y
    span = spectra.shape[2]
    lanes = spectra.shape[3]
    early = rim.shape[1]
    reach = early + 1
    z = lax.axis_index("chan")
    inp = lax.axis_index("inp")
    core = lax.rem(inp, 2)
    chip = lax.div(inp, 2)
    y = lax.rem(chip, grid_y)
    x = lax.div(chip, grid_y)
    here = ((x, y), (y, x))

    def wrap(index):
        return lax.rem(index + 4, 4)

    def device_of(part, u, v):
        first, second = (u, v) if part == 0 else (v, u)
        return (wrap(first) * grid_y + wrap(second)) * 2 + core

    partner = chip * 2 + 1 - core

    barrier = pltpu.get_barrier_semaphore()

    def greet_z(step, carry):
        pl.semaphore_signal(
            barrier, inc=1, device_id={"chan": lax.rem(z + step, zs)}, device_id_type=MESH
        )
        return carry

    lax.fori_loop(1, zs, greet_z, 0)
    for du, dv in ((1, 0), (-1, 0), (0, 1), (0, -1)):
        pl.semaphore_signal(
            barrier, inc=1, device_id={"inp": device_of(0, x + du, y + dv)}, device_id_type=MESH
        )
    pl.semaphore_signal(barrier, inc=1, device_id={"inp": partner}, device_id_type=MESH)

    for part in (0, 1):
        samples = pl.ds(part * zs, zs)
        frames[0:early, samples] = rim[part].astype(jnp.float32).astype(jnp.bfloat16)
        frames[early:, samples] = volts[part].astype(jnp.float32).astype(jnp.bfloat16)
    later_first = [taps[k : k + 1] for k in range(early, -1, -1) for part in (0, 1)]
    weights = table[...] * jnp.concatenate(later_first, 1)
    coarse = weights.astype(jnp.bfloat16)
    rest = weights - coarse.astype(jnp.float32)
    middle = rest.astype(jnp.bfloat16)
    fine = (rest - middle.astype(jnp.float32)).astype(jnp.bfloat16)
    pieces = jnp.concatenate([coarse, middle, fine], 0)
    outs = 2 * zs

    def channelize(s, carry):
        pair = [frames[pl.ds(first, reach)].reshape(reach * outs, lanes) for first in (s, s + span // 2)]
        product = jnp.dot(
            pieces, jnp.concatenate(pair, 1), preferred_element_type=jnp.float32
        )
        total = (product[:outs] + (product[outs : 2 * outs] + product[2 * outs :])) * volt_scale
        for n, first in enumerate((s, s + span // 2)):
            stage_f32[pl.ds(first, outs, stride=span), :] = total[:, n * lanes : (n + 1) * lanes]
        return carry

    lax.fori_loop(0, span // 2, channelize, 0, unroll=2)
    spectra[...] = stage_f32[...].reshape(spectra.shape).astype(jnp.bfloat16)
    out[...] = jnp.zeros_like(out)
    pl.semaphore_wait(barrier, zs + 4)

    def own_block(source, part):
        u, v = here[part]
        return store.at[source, core, part, v, u]

    for part in (0, 1):
        pltpu.make_async_copy(spectra.at[z, part], own_block(z, part), sem_a.at[z]).start()

    def offset_of(turn):
        return lax.div(turn + 1, 2) * (2 * lax.rem(turn, 2) - 1)

    def corner_turn(turn, carry):
        target = lax.rem(z + offset_of(turn) + zs, zs)
        for part in (0, 1):
            pltpu.make_async_remote_copy(
                src_ref=spectra.at[target, part], dst_ref=own_block(z, part),
                send_sem=send_a, recv_sem=sem_a.at[z],
                device_id={"chan": target}, device_id_type=MESH,
            ).start()
        return carry

    lax.fori_loop(1, zs, corner_turn, 0)

    def source_of(turn):
        return lax.rem(z + offset_of(turn) + zs, zs)

    def arrive(sem, ref):
        pltpu.make_async_copy(ref, ref, sem).wait()

    def give(ref, target, send, recv):
        pltpu.make_async_remote_copy(
            src_ref=ref, dst_ref=ref, send_sem=send, recv_sem=recv,
            device_id={"inp": target}, device_id_type=MESH,
        ).start()

    def stage(t, action):
        @pl.when(jnp.logical_and(t >= 0, t < zs))
        def _():
            action(t, source_of(t))

    def way_of(t, part):
        return 1 - 2 * lax.rem(t + part, 2)

    def step_a(t, k):
        arrive(sem_a.at[k], store.at[k, core, :, 0, 0])
        for part in (0, 1):
            u, v = here[part]
            for side in (1, -1):
                give(store.at[k, core, part, v, u], device_of(part, u + side, v), send_b.at[t], sem_b.at[t])

    def step_b(t, k):
        arrive(sem_b.at[t], store.at[k, core, :, 0, pl.ds(0, 2)])
        for part in (0, 1):
            u, v = here[part]
            way = way_of(t, part)
            give(
                store.at[k, core, part, v, wrap(u - way)], device_of(part, u + way, v),
                send_b.at[t], sem_c.at[t],
            )

    def give_row(t, k, part, row, way, recv):
        u, v = here[part]
        give(store.at[k, core, part, wrap(row)], device_of(part, u, v + way), send_r.at[t], recv)

    def share_row(t, k, part, row):
        give(store.at[k, core, part, wrap(row)], partner, send_p.at[t], sem_p.at[t])

    def step_c(t, k):
        arrive(sem_c.at[t], store.at[k, core, :, 0, 0])
        for part in (0, 1):
            give_row(t, k, part, here[part][1], way_of(t, part), sem_d.at[t])

    def step_f(t, k):
        for part in (0, 1):
            give_row(t, k, part, here[part][1], -way_of(t, part), sem_f.at[t])

    def step_d(t, k):
        arrive(sem_d.at[t], store.at[k, core, :, 0])
        for part in (0, 1):
            v = here[part][1]
            way = way_of(t, part)
            give_row(t, k, part, v - way, way, sem_g.at[t])
        for part in (0, 1):
            v = here[part][1]
            share_row(t, k, part, v)
            share_row(t, k, part, v - way_of(t, part))

    def step_e(t, k):
        arrive(sem_f.at[t], store.at[k, core, :, 0])
        arrive(sem_g.at[t], store.at[k, core, :, 0])
        for part in (0, 1):
            v = here[part][1]
            share_row(t, k, part, v + way_of(t, part))
            share_row(t, k, part, v + 2)

    def correlate(t, quarter):
        ks = [source_of(t + step) for step in range(4)]

        @pl.when(quarter == 0)
        def _():
            for step, k in enumerate(ks):
                arrive(sem_p.at[t + step], store.at[k, 1 - core])
            depth = 4 * span
            mine = []
            for part in (0, 1):
                u, v = here[part]
                both = jnp.concatenate([store[k, core, part, v, u] for k in ks], 0)
                mine.append(both.astype(jnp.float32).T)
            real, imag = mine
            rows[:lanes, :depth] = real.astype(jnp.bfloat16)
            rows[:lanes, depth:] = imag.astype(jnp.bfloat16)
            rows[lanes:, :depth] = imag.astype(jnp.bfloat16)
            rows[lanes:, depth:] = (-real).astype(jnp.bfloat16)

        left = rows[...]
        for second in range(grid_y):
            block = jnp.concatenate(
                [
                    jnp.concatenate([store[k, c, 0, second, quarter] for c in (0, 1)], 1) for k in ks
                ]
                + [
                    jnp.concatenate([store[k, c, 1, quarter, second] for c in (0, 1)], 1) for k in ks
                ],
                0,
            )
            product = jnp.dot(left, block, preferred_element_type=jnp.float32)
            begin = (quarter * grid_y + second) * (2 * lanes)
            columns = pl.ds(pl.multiple_of(begin, 2 * lanes), 2 * lanes)
            out[0, 0, :, columns] += product[:lanes]
            out[0, 1, :, columns] += product[lanes:]

    def iteration(it, carry):
        stage(it, step_a)
        stage(it - LAGS[0], step_b)
        stage(it - LAGS[1], step_c)
        stage(it - LAGS[3], step_f)
        late = it - LAGS[5]

        @pl.when(jnp.logical_and(late >= 0, late < zs))
        def _():
            quarter = lax.rem(late, 4)
            correlate(late - quarter, quarter)

        stage(it - LAGS[2], step_d)
        stage(it - LAGS[4], step_e)
        return carry

    lax.fori_loop(0, zs + LAGS[5], iteration, 0)

    arrive(send_a, spectra.at[pl.ds(0, zs - 1)])

    def drain(t, carry):
        arrive(send_b.at[t], store.at[0, 0, :, 0, pl.ds(0, 3)])
        arrive(send_r.at[t], store.at[0, 0, :, pl.ds(0, 3)])
        arrive(send_p.at[t], store.at[0, 0])
        return carry

    lax.fori_loop(0, zs, drain, 0)


def exchange(volts, rim, taps):
    parts, span, zs, lanes = volts.shape
    early = rim.shape[1]
    chips = grid_x * grid_y
    table = dft_rows(zs, early + 1)
    dma = pltpu.SemaphoreType.DMA
    return pl.pallas_call(
        functools.partial(exchange_kernel, zs),
        out_shape=jax.ShapeDtypeStruct((1, 2, lanes, 2 * chips * lanes), jnp.float32),
        in_specs=[pl.BlockSpec(memory_space=pltpu.VMEM)] * 4,
        out_specs=pl.BlockSpec(memory_space=pltpu.VMEM),
        scratch_shapes=[
            pltpu.VMEM((zs, 2, 2, grid_y, grid_x, span, lanes), jnp.bfloat16),
            pltpu.VMEM((2 * lanes, 8 * span), jnp.bfloat16),
            pltpu.VMEM((early + span, 2 * zs, lanes), jnp.bfloat16),
            pltpu.VMEM((2 * zs * span, lanes), jnp.float32),
            pltpu.VMEM((zs, 2, span, lanes), jnp.bfloat16),
        ]
        + [dma((zs,))] * 7
        + [dma]
        + [dma((zs,))] * 3,
        compiler_params=pltpu.CompilerParams(
            collective_id=0, has_side_effects=True, vmem_limit_bytes=40 * 1024 * 1024
        ),
    )(volts, rim, taps, table)


def body(voltages, fir_taps):
    frames = voltages.shape[1]
    tap_count = fir_taps.shape[0]
    rim = passed_along(voltages[:, frames - (tap_count - 1) :], "chan", 1)
    norm_factor = 1.0 / (frames * lax.axis_size("chan"))
    return exchange(voltages, rim, fir_taps) * norm_factor


def solution(mesh):
    placed = (P(None, "chan", None, "inp"), P())
    return jax.shard_map(
        body, mesh=mesh, in_specs=placed, out_specs=P("chan", None, "inp", None), check_vma=False
    )
```

```python
import functools
import math

import jax
import jax.numpy as jnp
from jax import lax
from jax.experimental import pallas as pl
from jax.experimental.pallas import tpu as pltpu
from jax.sharding import PartitionSpec as P


volt_scale = 1.0 / 256.0
LAGS = (2, 4, 6, 6, 8, 12)
DIRECT = 2
grid_x = 4
grid_y = 4
MESH = pl.DeviceIdType.MESH


def dft_entries(count, tap_count):
    shape = (2 * count, 2 * count * tap_count)
    row = lax.broadcasted_iota(jnp.int32, shape, 0)
    column = lax.broadcasted_iota(jnp.int32, shape, 1)
    channel, imag_out = row // 2, row % 2
    imag_in, sample = (column // count) % 2, column % count
    phase = (channel * sample + (imag_out - imag_in + 4) * (count // 4)) % count
    entries = jnp.zeros(shape, jnp.float32)
    for step in range(count):
        entries = jnp.where(phase == step, math.cos(2.0 * math.pi * step / count), entries)
    return entries


def exchange_kernel(
    zs, volts_far, taps_far, out_far,
    out, store, rows, frames, stage_f32, spectra, volts, taps, rim, sem_load, sem_rim, sem_out,
    sem_a, sem_b, sem_c, sem_d, sem_f, sem_g, sem_p, send_a, send_b, send_r, send_p,
):
    chips = grid_x * grid_y
    span = spectra.shape[2]
    lanes = spectra.shape[3]
    reach = taps.shape[0]
    early = reach - 1
    z = lax.axis_index("chan")
    inp = lax.axis_index("inp")
    core = lax.rem(inp, 2)
    chip = lax.div(inp, 2)
    y = lax.rem(chip, grid_y)
    x = lax.div(chip, grid_y)
    here = ((x, y), (y, x))

    def wrap(index):
        return lax.rem(index + 4, 4)

    def device_of(part, u, v):
        first, second = (u, v) if part == 0 else (v, u)
        return (wrap(first) * grid_y + wrap(second)) * 2 + core

    partner = chip * 2 + 1 - core

    loads = (
        pltpu.make_async_copy(volts_far, volts, sem_load.at[0]),
        pltpu.make_async_copy(taps_far, taps, sem_load.at[1]),
    )
    for copy in loads:
        copy.start()

    barrier = pltpu.get_barrier_semaphore()

    def greet_z(step, carry):
        pl.semaphore_signal(
            barrier, inc=1, device_id={"chan": lax.rem(z + step, zs)}, device_id_type=MESH
        )
        return carry

    lax.fori_loop(1, zs, greet_z, 0)
    for du, dv in ((1, 0), (-1, 0), (2, 0), (0, 1), (0, -1), (0, 2)):
        pl.semaphore_signal(
            barrier, inc=1, device_id={"inp": device_of(0, x + du, y + dv)}, device_id_type=MESH
        )
    pl.semaphore_signal(barrier, inc=1, device_id={"inp": partner}, device_id_type=MESH)

    for copy in loads:
        copy.wait()
    for part in (0, 1):
        frames[early:, part * zs : (part + 1) * zs] = (
            volts[part].astype(jnp.float32).astype(jnp.bfloat16)
        )
    later_first = [taps[k : k + 1] for k in range(early, -1, -1) for part in (0, 1)]
    weights = dft_entries(zs, reach) * jnp.concatenate(later_first, 1)
    coarse = weights.astype(jnp.bfloat16)
    rest = weights - coarse.astype(jnp.float32)
    middle = rest.astype(jnp.bfloat16)
    fine = (rest - middle.astype(jnp.float32)).astype(jnp.bfloat16)
    pieces = jnp.concatenate([coarse, middle, fine], 0)
    outs = 2 * zs

    def channelize(*spots):
        columns = [frames[pl.ds(s, reach)].reshape(reach * outs, lanes) for s in spots]
        product = jnp.dot(pieces, jnp.concatenate(columns, 1), preferred_element_type=jnp.float32)
        total = (product[:outs] + (product[outs : 2 * outs] + product[2 * outs :])) * volt_scale
        for n, s in enumerate(spots):
            stage_f32[pl.ds(s, outs, stride=span), :] = total[:, n * lanes : (n + 1) * lanes]

    def channelize_pair(step, carry):
        channelize(early + step, early + step + half)
        return carry

    half = (span - early) // 2
    lax.fori_loop(0, half, channelize_pair, 0, unroll=2)
    if early + 2 * half < span:
        channelize(span - 1)
    lead = min(16, span // 2)
    staged = stage_f32[: outs * span].reshape(spectra.shape)
    spectra[:, :, lead:] = staged[:, :, lead:].astype(jnp.bfloat16)
    out[...] = jnp.zeros_like(out)
    pl.semaphore_wait(barrier, zs + 6)

    rim_copy = pltpu.make_async_remote_copy(
        src_ref=volts.at[:, pl.ds(span - early, early)], dst_ref=rim,
        send_sem=sem_rim.at[0], recv_sem=sem_rim.at[1],
        device_id={"chan": lax.rem(z + 1, zs)}, device_id_type=MESH,
    )
    rim_copy.start()
    rim_copy.wait()
    for part in (0, 1):
        before = rim[part] * jnp.minimum(z, 1)
        frames[0:early, part * zs : (part + 1) * zs] = before.astype(jnp.float32).astype(jnp.bfloat16)
    for first in range(0, early, 2):
        channelize(*range(first, min(first + 2, early)))
    staged = stage_f32[: outs * span].reshape(spectra.shape)
    spectra[:, :, :lead] = staged[:, :, :lead].astype(jnp.bfloat16)

    def own_block(source, part):
        u, v = here[part]
        return store.at[source, core, part, v, u]

    for part in (0, 1):
        pltpu.make_async_copy(spectra.at[z, part], own_block(z, part), sem_a.at[z]).start()

    def offset_of(turn):
        return lax.div(turn + 1, 2) * (2 * lax.rem(turn, 2) - 1)

    def corner_turn(turn, carry):
        target = lax.rem(z + offset_of(turn) + zs, zs)
        for part in (0, 1):
            pltpu.make_async_remote_copy(
                src_ref=spectra.at[target, part], dst_ref=own_block(z, part),
                send_sem=send_a, recv_sem=sem_a.at[z],
                device_id={"chan": target}, device_id_type=MESH,
            ).start()
        return carry

    lax.fori_loop(1, zs, corner_turn, 0)

    def source_of(turn):
        return lax.rem(z + offset_of(turn) + zs, zs)

    def arrive(sem, ref):
        pltpu.make_async_copy(ref, ref, sem).wait()

    def give(ref, target, send, recv):
        pltpu.make_async_remote_copy(
            src_ref=ref, dst_ref=ref, send_sem=send, recv_sem=recv,
            device_id={"inp": target}, device_id_type=MESH,
        ).start()

    def stage(t, action):
        @pl.when(jnp.logical_and(t >= 0, t < zs))
        def _():
            action(t, source_of(t))

    def way_of(t, part):
        return 1 - 2 * lax.rem(t + part, 2)

    def step_a(t, k):
        arrive(sem_a.at[k], store.at[k, core, :, 0, 0])
        for part in (0, 1):
            u, v = here[part]
            for side in (1, -1):
                give(store.at[k, core, part, v, u], device_of(part, u + side, v), send_b.at[t], sem_b.at[t])

        @pl.when(t >= zs - DIRECT)
        def _():
            for part in (0, 1):
                u, v = here[part]
                give(store.at[k, core, part, v, u], device_of(part, u + 2, v), send_b.at[t], sem_c.at[t])

    def step_b(t, k):
        arrive(sem_b.at[t], store.at[k, core, :, 0, pl.ds(0, 2)])

        @pl.when(t < zs - DIRECT)
        def _():
            for part in (0, 1):
                u, v = here[part]
                way = way_of(t, part)
                give(
                    store.at[k, core, part, v, wrap(u - way)], device_of(part, u + way, v),
                    send_b.at[t], sem_c.at[t],
                )

    def give_row(t, k, part, row, way, recv):
        u, v = here[part]
        give(store.at[k, core, part, wrap(row)], device_of(part, u, v + way), send_r.at[t], recv)

    def share_row(t, k, part, row):
        give(store.at[k, core, part, wrap(row)], partner, send_p.at[t], sem_p.at[t])

    def step_c(t, k):
        arrive(sem_c.at[t], store.at[k, core, :, 0, 0])
        for part in (0, 1):
            give_row(t, k, part, here[part][1], way_of(t, part), sem_d.at[t])

        @pl.when(t >= zs - DIRECT)
        def _():
            for part in (0, 1):
                give_row(t, k, part, here[part][1], 2, sem_g.at[t])

    def step_f(t, k):
        for part in (0, 1):
            give_row(t, k, part, here[part][1], -way_of(t, part), sem_f.at[t])

    def step_d(t, k):
        arrive(sem_d.at[t], store.at[k, core, :, 0])

        @pl.when(t < zs - DIRECT)
        def _():
            for part in (0, 1):
                v = here[part][1]
                way = way_of(t, part)
                give_row(t, k, part, v - way, way, sem_g.at[t])

        for part in (0, 1):
            v = here[part][1]
            share_row(t, k, part, v)
            share_row(t, k, part, v - way_of(t, part))

    def step_e(t, k):
        arrive(sem_f.at[t], store.at[k, core, :, 0])
        arrive(sem_g.at[t], store.at[k, core, :, 0])
        for part in (0, 1):
            v = here[part][1]
            share_row(t, k, part, v + way_of(t, part))
            share_row(t, k, part, v + 2)

    def correlate(t, quarter):
        ks = [source_of(t + step) for step in range(4)]

        @pl.when(quarter == 0)
        def _():
            for step, k in enumerate(ks):
                arrive(sem_p.at[t + step], store.at[k, 1 - core])
            depth = 4 * span
            mine = []
            for part in (0, 1):
                u, v = here[part]
                both = jnp.concatenate([store[k, core, part, v, u] for k in ks], 0)
                mine.append(both.astype(jnp.float32).T)
            real, imag = mine
            rows[:lanes, :depth] = real.astype(jnp.bfloat16)
            rows[:lanes, depth:] = imag.astype(jnp.bfloat16)
            rows[lanes:, :depth] = imag.astype(jnp.bfloat16)
            rows[lanes:, depth:] = (-real).astype(jnp.bfloat16)

        left = rows[...]
        for second in range(grid_y):
            block = jnp.concatenate(
                [
                    jnp.concatenate([store[k, c, 0, second, quarter] for c in (0, 1)], 1) for k in ks
                ]
                + [
                    jnp.concatenate([store[k, c, 1, quarter, second] for c in (0, 1)], 1) for k in ks
                ],
                0,
            )
            product = jnp.dot(left, block, preferred_element_type=jnp.float32)
            begin = (quarter * grid_y + second) * (2 * lanes)
            columns = pl.ds(pl.multiple_of(begin, 2 * lanes), 2 * lanes)
            out[0, :, columns] += product[:lanes]
            out[1, :, columns] += product[lanes:]

    def out_copy(quarter):
        width = 2 * grid_y * lanes
        columns = pl.ds(pl.multiple_of(quarter * width, width), width)
        return pltpu.make_async_copy(
            out.at[:, :, columns], out_far.at[0, :, :, columns], sem_out.at[quarter]
        )

    def iteration(it, carry):
        stage(it, step_a)
        stage(it - LAGS[0], step_b)
        stage(it - LAGS[1], step_c)
        stage(it - LAGS[3], step_f)
        late = it - LAGS[5]

        @pl.when(jnp.logical_and(late >= 0, late < zs))
        def _():
            quarter = lax.rem(late, 4)
            correlate(late - quarter, quarter)

            @pl.when(late >= zs - 4)
            def _():
                out_copy(quarter).start()

        stage(it - LAGS[2], step_d)
        stage(it - LAGS[4], step_e)
        return carry

    lax.fori_loop(0, zs + LAGS[5], iteration, 0)

    arrive(send_a, spectra.at[pl.ds(0, zs - 1)])

    def drain(t, carry):
        arrive(send_b.at[t], store.at[0, 0, :, 0, pl.ds(0, 3)])
        arrive(send_r.at[t], store.at[0, 0, :, pl.ds(0, 3)])
        arrive(send_p.at[t], store.at[0, 0])
        return carry

    lax.fori_loop(0, zs, drain, 0)
    for quarter in range(4):
        out_copy(quarter).wait()


def exchange(volts, taps):
    parts, span, zs, lanes = volts.shape
    tap_count = taps.shape[0]
    chips = grid_x * grid_y
    result = (2, lanes, 2 * chips * lanes)
    dma = pltpu.SemaphoreType.DMA
    return pl.pallas_call(
        functools.partial(exchange_kernel, zs),
        out_shape=jax.ShapeDtypeStruct((1,) + result, jnp.float32),
        in_specs=[pl.BlockSpec(memory_space=pl.ANY)] * 2,
        out_specs=pl.BlockSpec(memory_space=pl.ANY),
        scratch_shapes=[
            pltpu.VMEM(result, jnp.float32),
            pltpu.VMEM((zs, 2, 2, grid_y, grid_x, span, lanes), jnp.bfloat16),
            pltpu.VMEM((2 * lanes, 8 * span), jnp.bfloat16),
            pltpu.VMEM((tap_count - 1 + span, 2 * zs, lanes), jnp.bfloat16),
            pltpu.VMEM(((2 * zs + 1) * span, lanes), jnp.float32),
            pltpu.VMEM((zs, 2, span, lanes), jnp.bfloat16),
            pltpu.VMEM(volts.shape, volts.dtype),
            pltpu.VMEM(taps.shape, taps.dtype),
            pltpu.VMEM((2, tap_count - 1, zs, lanes), volts.dtype),
            dma((2,)),
            dma((2,)),
            dma((4,)),
        ]
        + [dma((zs,))] * 7
        + [dma]
        + [dma((zs,))] * 3,
        compiler_params=pltpu.CompilerParams(
            collective_id=0, has_side_effects=True, vmem_limit_bytes=58 * 1024 * 1024
        ),
    )(volts, taps)


def body(voltages, fir_taps):
    norm_factor = 1.0 / (voltages.shape[1] * lax.axis_size("chan"))
    return exchange(voltages, fir_taps) * norm_factor


def solution(mesh):
    placed = (P(None, "chan", None, "inp"), P())
    return jax.shard_map(
        body, mesh=mesh, in_specs=placed, out_specs=P("chan", None, "inp", None), check_vma=False
    )
```

```python
import functools
import math

import jax
import jax.numpy as jnp
from jax import lax
from jax.experimental import pallas as pl
from jax.experimental.pallas import tpu as pltpu
from jax.sharding import PartitionSpec as P


volt_scale = 1.0 / 256.0
LAGS = (2, 4, 6, 6, 9, 14)
grid_x = 4
grid_y = 4
MESH = pl.DeviceIdType.MESH


def dft_entries(count, tap_count):
    shape = (2 * count, 2 * count * tap_count)
    row = lax.broadcasted_iota(jnp.int32, shape, 0)
    column = lax.broadcasted_iota(jnp.int32, shape, 1)
    channel, imag_out = row // 2, row % 2
    imag_in, sample = (column // count) % 2, column % count
    phase = (channel * sample + (imag_out - imag_in + 4) * (count // 4)) % count
    entries = jnp.zeros(shape, jnp.float32)
    for step in range(count):
        entries = jnp.where(phase == step, math.cos(2.0 * math.pi * step / count), entries)
    return entries


def exchange_kernel(
    zs, volts, taps, out,
    store, rows, frames, stage_f32, spectra, rim, sem_rim,
    sem_a, sem_b, sem_c, sem_d, sem_f, sem_g, sem_p, send_a, send_b, send_r, send_p,
):
    chips = grid_x * grid_y
    span = spectra.shape[2]
    lanes = spectra.shape[3]
    reach = taps.shape[0]
    early = reach - 1
    z = lax.axis_index("chan")
    inp = lax.axis_index("inp")
    core = lax.rem(inp, 2)
    chip = lax.div(inp, 2)
    y = lax.rem(chip, grid_y)
    x = lax.div(chip, grid_y)
    here = ((x, y), (y, x))

    def wrap(index):
        return lax.rem(index + 4, 4)

    def device_of(part, u, v):
        first, second = (u, v) if part == 0 else (v, u)
        return (wrap(first) * grid_y + wrap(second)) * 2 + core

    partner = chip * 2 + 1 - core

    barrier = pltpu.get_barrier_semaphore()

    def greet_z(step, carry):
        pl.semaphore_signal(
            barrier, inc=1, device_id={"chan": lax.rem(z + step, zs)}, device_id_type=MESH
        )
        return carry

    lax.fori_loop(1, zs, greet_z, 0)
    for du, dv in ((1, 0), (-1, 0), (0, 1), (0, -1)):
        pl.semaphore_signal(
            barrier, inc=1, device_id={"inp": device_of(0, x + du, y + dv)}, device_id_type=MESH
        )
    pl.semaphore_signal(barrier, inc=1, device_id={"inp": partner}, device_id_type=MESH)

    for part in (0, 1):
        frames[early:, part * zs : (part + 1) * zs] = (
            volts[part].astype(jnp.float32).astype(jnp.bfloat16)
        )
    later_first = [taps[k : k + 1] for k in range(early, -1, -1) for part in (0, 1)]
    weights = dft_entries(zs, reach) * jnp.concatenate(later_first, 1)
    coarse = weights.astype(jnp.bfloat16)
    rest = weights - coarse.astype(jnp.float32)
    middle = rest.astype(jnp.bfloat16)
    fine = (rest - middle.astype(jnp.float32)).astype(jnp.bfloat16)
    pieces = jnp.concatenate([coarse, middle, fine], 0)
    outs = 2 * zs

    def channelize(*spots):
        columns = [frames[pl.ds(s, reach)].reshape(reach * outs, lanes) for s in spots]
        product = jnp.dot(pieces, jnp.concatenate(columns, 1), preferred_element_type=jnp.float32)
        total = (product[:outs] + (product[outs : 2 * outs] + product[2 * outs :])) * volt_scale
        for n, s in enumerate(spots):
            stage_f32[pl.ds(s, outs, stride=span), :] = total[:, n * lanes : (n + 1) * lanes]

    def channelize_pair(step, carry):
        channelize(early + step, early + step + half)
        return carry

    half = (span - early) // 2
    lax.fori_loop(0, half, channelize_pair, 0, unroll=2)
    if early + 2 * half < span:
        channelize(span - 1)
    lead = min(16, span // 2)
    staged = stage_f32[: outs * span].reshape(spectra.shape)
    spectra[:, :, lead:] = staged[:, :, lead:].astype(jnp.bfloat16)
    out[...] = jnp.zeros_like(out)
    pl.semaphore_wait(barrier, zs + 4)

    rim_copy = pltpu.make_async_remote_copy(
        src_ref=volts.at[:, pl.ds(span - early, early)], dst_ref=rim,
        send_sem=sem_rim.at[0], recv_sem=sem_rim.at[1],
        device_id={"chan": lax.rem(z + 1, zs)}, device_id_type=MESH,
    )
    rim_copy.start()
    rim_copy.wait()
    for part in (0, 1):
        before = rim[part] * jnp.minimum(z, 1)
        frames[0:early, part * zs : (part + 1) * zs] = before.astype(jnp.float32).astype(jnp.bfloat16)
    for first in range(0, early, 2):
        channelize(*range(first, min(first + 2, early)))
    staged = stage_f32[: outs * span].reshape(spectra.shape)
    spectra[:, :, :lead] = staged[:, :, :lead].astype(jnp.bfloat16)

    def own_block(source, part):
        u, v = here[part]
        return store.at[source, core, part, v, u]

    for part in (0, 1):
        pltpu.make_async_copy(spectra.at[z, part], own_block(z, part), sem_a.at[z]).start()

    def offset_of(turn):
        return lax.div(turn + 1, 2) * (2 * lax.rem(turn, 2) - 1)

    def corner_turn(turn, carry):
        target = lax.rem(z + offset_of(turn) + zs, zs)
        for part in (0, 1):
            pltpu.make_async_remote_copy(
                src_ref=spectra.at[target, part], dst_ref=own_block(z, part),
                send_sem=send_a, recv_sem=sem_a.at[z],
                device_id={"chan": target}, device_id_type=MESH,
            ).start()
        return carry

    lax.fori_loop(1, zs, corner_turn, 0)

    def source_of(turn):
        return lax.rem(z + offset_of(turn) + zs, zs)

    def arrive(sem, ref):
        pltpu.make_async_copy(ref, ref, sem).wait()

    def give(ref, target, send, recv):
        pltpu.make_async_remote_copy(
            src_ref=ref, dst_ref=ref, send_sem=send, recv_sem=recv,
            device_id={"inp": target}, device_id_type=MESH,
        ).start()

    def stage(t, action):
        @pl.when(jnp.logical_and(t >= 0, t < zs))
        def _():
            action(t, source_of(t))

    def way_of(t, part):
        return 1 - 2 * lax.rem(t + part, 2)

    def give_block(t, k, part, shift):
        u, v = here[part]
        give(
            store.at[k, core, part, v, wrap(u + shift)], device_of(part, u, v + way_of(t, part)),
            send_r.at[t], sem_d.at[t],
        )

    def step_a(t, k):
        arrive(sem_a.at[k], store.at[k, core, :, 0, 0])
        for part in (0, 1):
            u, v = here[part]
            for side in (1, -1):
                give(store.at[k, core, part, v, u], device_of(part, u + side, v), send_b.at[t], sem_b.at[t])
        for part in (0, 1):
            give_block(t, k, part, 0)

    def step_b(t, k):
        arrive(sem_b.at[t], store.at[k, core, :, 0, pl.ds(0, 2)])
        for part in (0, 1):
            u, v = here[part]
            way = way_of(t, part)
            give(
                store.at[k, core, part, v, wrap(u - way)], device_of(part, u + way, v),
                send_b.at[t], sem_c.at[t],
            )
        for shift in (1, -1):
            for part in (0, 1):
                give_block(t, k, part, shift)

    def give_row(t, k, part, row, way, recv):
        u, v = here[part]
        give(store.at[k, core, part, wrap(row)], device_of(part, u, v + way), send_r.at[t], recv)

    def share_row(t, k, part, row):
        give(store.at[k, core, part, wrap(row)], partner, send_p.at[t], sem_p.at[t])

    def step_c(t, k):
        arrive(sem_c.at[t], store.at[k, core, :, 0, 0])
        for part in (0, 1):
            give_block(t, k, part, 2)

    def step_f(t, k):
        for part in (0, 1):
            give_row(t, k, part, here[part][1], -way_of(t, part), sem_f.at[t])

    def step_d(t, k):
        arrive(sem_d.at[t], store.at[k, core, :, 0])
        for part in (0, 1):
            v = here[part][1]
            way = way_of(t, part)
            give_row(t, k, part, v - way, way, sem_g.at[t])
        for part in (0, 1):
            v = here[part][1]
            share_row(t, k, part, v)
            share_row(t, k, part, v - way_of(t, part))

    def step_e(t, k):
        arrive(sem_f.at[t], store.at[k, core, :, 0])
        arrive(sem_g.at[t], store.at[k, core, :, 0])
        for part in (0, 1):
            v = here[part][1]
            share_row(t, k, part, v + way_of(t, part))
            share_row(t, k, part, v + 2)

    def correlate(t, quarter):
        ks = [source_of(t + step) for step in range(4)]

        @pl.when(quarter == 0)
        def _():
            for step, k in enumerate(ks):
                arrive(sem_p.at[t + step], store.at[k, 1 - core])
            depth = 4 * span
            mine = []
            for part in (0, 1):
                u, v = here[part]
                both = jnp.concatenate([store[k, core, part, v, u] for k in ks], 0)
                mine.append(both.astype(jnp.float32).T)
            real, imag = mine
            rows[:lanes, :depth] = real.astype(jnp.bfloat16)
            rows[:lanes, depth:] = imag.astype(jnp.bfloat16)
            rows[lanes:, :depth] = imag.astype(jnp.bfloat16)
            rows[lanes:, depth:] = (-real).astype(jnp.bfloat16)

        left = rows[...]
        for second in range(grid_y):
            block = jnp.concatenate(
                [
                    jnp.concatenate([store[k, c, 0, second, quarter] for c in (0, 1)], 1) for k in ks
                ]
                + [
                    jnp.concatenate([store[k, c, 1, quarter, second] for c in (0, 1)], 1) for k in ks
                ],
                0,
            )
            product = jnp.dot(left, block, preferred_element_type=jnp.float32)
            begin = (quarter * grid_y + second) * (2 * lanes)
            columns = pl.ds(pl.multiple_of(begin, 2 * lanes), 2 * lanes)
            out[0, 0, :, columns] += product[:lanes]
            out[0, 1, :, columns] += product[lanes:]

    def iteration(it, carry):
        stage(it, step_a)
        stage(it - LAGS[0], step_b)
        stage(it - LAGS[1], step_c)
        stage(it - LAGS[3], step_f)
        late = it - LAGS[5]

        @pl.when(jnp.logical_and(late >= 0, late < zs))
        def _():
            quarter = lax.rem(late, 4)
            correlate(late - quarter, quarter)


        stage(it - LAGS[2], step_d)
        stage(it - LAGS[4], step_e)
        return carry

    lax.fori_loop(0, zs + LAGS[5], iteration, 0)

    arrive(send_a, spectra.at[pl.ds(0, zs - 1)])

    def drain(t, carry):
        arrive(send_b.at[t], store.at[0, 0, :, 0, pl.ds(0, 3)])
        arrive(send_r.at[t], store.at[0, 0, :, pl.ds(0, 3)])
        arrive(send_p.at[t], store.at[0, 0])
        return carry

    lax.fori_loop(0, zs, drain, 0)


def exchange(volts, taps):
    parts, span, zs, lanes = volts.shape
    tap_count = taps.shape[0]
    chips = grid_x * grid_y
    result = (2, lanes, 2 * chips * lanes)
    dma = pltpu.SemaphoreType.DMA
    return pl.pallas_call(
        functools.partial(exchange_kernel, zs),
        out_shape=jax.ShapeDtypeStruct((1,) + result, jnp.float32),
        in_specs=[pl.BlockSpec(memory_space=pltpu.VMEM)] * 2,
        out_specs=pl.BlockSpec(memory_space=pltpu.VMEM),
        scratch_shapes=[
            pltpu.VMEM((zs, 2, 2, grid_y, grid_x, span, lanes), jnp.bfloat16),
            pltpu.VMEM((2 * lanes, 8 * span), jnp.bfloat16),
            pltpu.VMEM((tap_count - 1 + span, 2 * zs, lanes), jnp.bfloat16),
            pltpu.VMEM(((2 * zs + 1) * span, lanes), jnp.float32),
            pltpu.VMEM((zs, 2, span, lanes), jnp.bfloat16),
            pltpu.VMEM((2, tap_count - 1, zs, lanes), volts.dtype),
            dma((2,)),
        ]
        + [dma((zs,))] * 7
        + [dma]
        + [dma((zs,))] * 3,
        compiler_params=pltpu.CompilerParams(
            collective_id=0, has_side_effects=True, vmem_limit_bytes=40 * 1024 * 1024
        ),
    )(volts, taps)


def body(voltages, fir_taps):
    norm_factor = 1.0 / (voltages.shape[1] * lax.axis_size("chan"))
    return exchange(voltages, fir_taps) * norm_factor


def solution(mesh):
    placed = (P(None, "chan", None, "inp"), P())
    return jax.shard_map(
        body, mesh=mesh, in_specs=placed, out_specs=P("chan", None, "inp", None), check_vma=False
    )
```

```python
import functools
import math

import jax
import jax.numpy as jnp
from jax import lax
from jax.experimental import pallas as pl
from jax.experimental.pallas import tpu as pltpu
from jax.sharding import PartitionSpec as P


volt_scale = 1.0 / 256.0
LAGS = (2, 4, 6, 6, 9, 13)
grid_x = 4
grid_y = 4
MESH = pl.DeviceIdType.MESH


def dft_entries(count, tap_count):
    shape = (2 * count, 2 * count * tap_count)
    row = lax.broadcasted_iota(jnp.int32, shape, 0)
    column = lax.broadcasted_iota(jnp.int32, shape, 1)
    channel, imag_out = row // 2, row % 2
    imag_in, sample = (column // count) % 2, column % count
    phase = (channel * sample + (imag_out - imag_in + 4) * (count // 4)) % count
    entries = jnp.zeros(shape, jnp.float32)
    for step in range(count):
        entries = jnp.where(phase == step, math.cos(2.0 * math.pi * step / count), entries)
    return entries


def exchange_kernel(
    zs, volts, taps, out,
    store, rows, last_rows, frames, stage_f32, spectra, rim, sem_rim,
    sem_a, sem_b, sem_c, sem_d, sem_f, sem_g, sem_p, send_a, send_b, send_r, send_p,
):
    chips = grid_x * grid_y
    span = spectra.shape[2]
    lanes = spectra.shape[3]
    reach = taps.shape[0]
    early = reach - 1
    z = lax.axis_index("chan")
    inp = lax.axis_index("inp")
    core = lax.rem(inp, 2)
    chip = lax.div(inp, 2)
    y = lax.rem(chip, grid_y)
    x = lax.div(chip, grid_y)
    here = ((x, y), (y, x))

    def wrap(index):
        return lax.rem(index + 4, 4)

    def device_of(part, u, v):
        first, second = (u, v) if part == 0 else (v, u)
        return (wrap(first) * grid_y + wrap(second)) * 2 + core

    partner = chip * 2 + 1 - core

    barrier = pltpu.get_barrier_semaphore()

    def greet_z(step, carry):
        pl.semaphore_signal(
            barrier, inc=1, device_id={"chan": lax.rem(z + step, zs)}, device_id_type=MESH
        )
        return carry

    lax.fori_loop(1, zs, greet_z, 0)
    for du, dv in ((1, 0), (-1, 0), (0, 1), (0, -1)):
        pl.semaphore_signal(
            barrier, inc=1, device_id={"inp": device_of(0, x + du, y + dv)}, device_id_type=MESH
        )
    pl.semaphore_signal(barrier, inc=1, device_id={"inp": partner}, device_id_type=MESH)

    for part in (0, 1):
        frames[early:, part * zs : (part + 1) * zs] = (
            volts[part].astype(jnp.float32).astype(jnp.bfloat16)
        )
    later_first = [taps[k : k + 1] for k in range(early, -1, -1) for part in (0, 1)]
    weights = dft_entries(zs, reach) * jnp.concatenate(later_first, 1)
    coarse = weights.astype(jnp.bfloat16)
    rest = weights - coarse.astype(jnp.float32)
    middle = rest.astype(jnp.bfloat16)
    fine = (rest - middle.astype(jnp.float32)).astype(jnp.bfloat16)
    pieces = jnp.concatenate([coarse, middle, fine], 0)
    outs = 2 * zs

    def channelize(*spots):
        columns = [frames[pl.ds(s, reach)].reshape(reach * outs, lanes) for s in spots]
        product = jnp.dot(pieces, jnp.concatenate(columns, 1), preferred_element_type=jnp.float32)
        total = (product[:outs] + (product[outs : 2 * outs] + product[2 * outs :])) * volt_scale
        for n, s in enumerate(spots):
            stage_f32[pl.ds(s, outs, stride=span), :] = total[:, n * lanes : (n + 1) * lanes]

    def channelize_pair(step, carry):
        channelize(early + step, early + step + half)
        return carry

    half = (span - early) // 2
    lax.fori_loop(0, half, channelize_pair, 0, unroll=2)
    if early + 2 * half < span:
        channelize(span - 1)
    lead = min(16, span // 2)
    staged = stage_f32[: outs * span].reshape(spectra.shape)
    spectra[:, :, lead:] = staged[:, :, lead:].astype(jnp.bfloat16)
    out[...] = jnp.zeros_like(out)
    pl.semaphore_wait(barrier, zs + 4)

    rim_copy = pltpu.make_async_remote_copy(
        src_ref=volts.at[:, pl.ds(span - early, early)], dst_ref=rim,
        send_sem=sem_rim.at[0], recv_sem=sem_rim.at[1],
        device_id={"chan": lax.rem(z + 1, zs)}, device_id_type=MESH,
    )
    rim_copy.start()
    rim_copy.wait()
    for part in (0, 1):
        before = rim[part] * jnp.minimum(z, 1)
        frames[0:early, part * zs : (part + 1) * zs] = before.astype(jnp.float32).astype(jnp.bfloat16)
    for first in range(0, early, 2):
        channelize(*range(first, min(first + 2, early)))
    staged = stage_f32[: outs * span].reshape(spectra.shape)
    spectra[:, :, :lead] = staged[:, :, :lead].astype(jnp.bfloat16)

    def own_block(source, part):
        u, v = here[part]
        return store.at[source, core, part, v, u]

    for part in (0, 1):
        pltpu.make_async_copy(spectra.at[z, part], own_block(z, part), sem_a.at[z]).start()

    def offset_of(turn):
        return lax.div(turn + 1, 2) * (2 * lax.rem(turn, 2) - 1)

    def corner_turn(turn, carry):
        target = lax.rem(z + offset_of(turn) + zs, zs)
        for part in (0, 1):
            pltpu.make_async_remote_copy(
                src_ref=spectra.at[target, part], dst_ref=own_block(z, part),
                send_sem=send_a, recv_sem=sem_a.at[z],
                device_id={"chan": target}, device_id_type=MESH,
            ).start()
        return carry

    lax.fori_loop(1, zs, corner_turn, 0)

    def source_of(turn):
        return lax.rem(z + offset_of(turn) + zs, zs)

    def arrive(sem, ref):
        pltpu.make_async_copy(ref, ref, sem).wait()

    def give(ref, target, send, recv):
        pltpu.make_async_remote_copy(
            src_ref=ref, dst_ref=ref, send_sem=send, recv_sem=recv,
            device_id={"inp": target}, device_id_type=MESH,
        ).start()

    def stage(t, action):
        @pl.when(jnp.logical_and(t >= 0, t < zs))
        def _():
            action(t, source_of(t))

    def way_of(t, part):
        return 1 - 2 * lax.rem(t + part, 2)

    def give_block(t, k, part, shift):
        u, v = here[part]
        give(
            store.at[k, core, part, v, wrap(u + shift)], device_of(part, u, v + way_of(t, part)),
            send_r.at[t], sem_d.at[t],
        )

    def step_a(t, k):
        arrive(sem_a.at[k], store.at[k, core, :, 0, 0])
        for part in (0, 1):
            u, v = here[part]
            for side in (1, -1):
                give(store.at[k, core, part, v, u], device_of(part, u + side, v), send_b.at[t], sem_b.at[t])
        for part in (0, 1):
            give_block(t, k, part, 0)

    def step_b(t, k):
        arrive(sem_b.at[t], store.at[k, core, :, 0, pl.ds(0, 2)])
        for part in (0, 1):
            u, v = here[part]
            way = way_of(t, part)
            give(
                store.at[k, core, part, v, wrap(u - way)], device_of(part, u + way, v),
                send_b.at[t], sem_c.at[t],
            )
        for shift in (1, -1):
            for part in (0, 1):
                give_block(t, k, part, shift)

    def give_row(t, k, part, row, way, recv):
        u, v = here[part]
        give(store.at[k, core, part, wrap(row)], device_of(part, u, v + way), send_r.at[t], recv)

    def share_row(t, k, part, row):
        give(store.at[k, core, part, wrap(row)], partner, send_p.at[t], sem_p.at[t])

    def step_c(t, k):
        arrive(sem_c.at[t], store.at[k, core, :, 0, 0])
        for part in (0, 1):
            give_block(t, k, part, 2)

    def step_f(t, k):
        for part in (0, 1):
            give_row(t, k, part, here[part][1], -way_of(t, part), sem_f.at[t])

    def step_d(t, k):
        arrive(sem_d.at[t], store.at[k, core, :, 0])
        for part in (0, 1):
            v = here[part][1]
            way = way_of(t, part)
            give_row(t, k, part, v - way, way, sem_g.at[t])
        for part in (0, 1):
            v = here[part][1]
            share_row(t, k, part, v)
            share_row(t, k, part, v - way_of(t, part))

    def step_e(t, k):
        arrive(sem_f.at[t], store.at[k, core, :, 0])
        arrive(sem_g.at[t], store.at[k, core, :, 0])
        for part in (0, 1):
            v = here[part][1]
            share_row(t, k, part, v + way_of(t, part))
            share_row(t, k, part, v + 2)

    def correlate(t, count, quarter, rows):
        ks = [source_of(t + step) for step in range(count)]

        @pl.when(quarter == 0)
        def _():
            for step, k in enumerate(ks):
                arrive(sem_p.at[t + step], store.at[k, 1 - core])
            depth = count * span
            mine = []
            for part in (0, 1):
                u, v = here[part]
                both = jnp.concatenate([store[k, core, part, v, u] for k in ks], 0)
                mine.append(both.astype(jnp.float32).T)
            real, imag = mine
            rows[:lanes, :depth] = real.astype(jnp.bfloat16)
            rows[:lanes, depth:] = imag.astype(jnp.bfloat16)
            rows[lanes:, :depth] = imag.astype(jnp.bfloat16)
            rows[lanes:, depth:] = (-real).astype(jnp.bfloat16)

        left = rows[...]
        for second in range(grid_y):
            block = jnp.concatenate(
                [
                    jnp.concatenate([store[k, c, 0, second, quarter] for c in (0, 1)], 1) for k in ks
                ]
                + [
                    jnp.concatenate([store[k, c, 1, quarter, second] for c in (0, 1)], 1) for k in ks
                ],
                0,
            )
            product = jnp.dot(left, block, preferred_element_type=jnp.float32)
            begin = (quarter * grid_y + second) * (2 * lanes)
            columns = pl.ds(pl.multiple_of(begin, 2 * lanes), 2 * lanes)
            out[0, 0, :, columns] += product[:lanes]
            out[0, 1, :, columns] += product[lanes:]

    def settle(t, k):
        arrive(send_b.at[t], store.at[0, 0, :, 0, pl.ds(0, 3)])
        arrive(send_r.at[t], store.at[0, 0, :, pl.ds(0, 3)])
        arrive(send_p.at[t], store.at[0, 0])

    def finish(t):
        def one_quarter(quarter, carry):
            correlate(t, 2, quarter, last_rows)
            return carry

        return one_quarter

    def iteration(it, carry):
        stage(it, step_a)
        stage(it - LAGS[0], step_b)
        stage(it - LAGS[1], step_c)
        stage(it - LAGS[3], step_f)
        late = it - LAGS[5]

        @pl.when(jnp.logical_and(late >= 0, late < zs - 4))
        def _():
            quarter = lax.rem(late, 4)
            correlate(late - quarter, 4, quarter, rows)

        ending = it - (zs + LAGS[4] - 2)

        @pl.when(ending >= 0)
        def _():
            lax.fori_loop(2 * ending, 2 * ending + 2, finish(zs - 4), 0)

        stage(it - LAGS[2], step_d)
        stage(it - LAGS[4], step_e)
        stage(it - LAGS[4] - 2, settle)
        return carry

    lax.fori_loop(0, zs + LAGS[4], iteration, 0)
    arrive(send_a, spectra.at[pl.ds(0, zs - 1)])
    lax.fori_loop(0, 4, finish(zs - 2), 0)
    for t in (zs - 2, zs - 1):
        settle(t, 0)


def exchange(volts, taps):
    parts, span, zs, lanes = volts.shape
    tap_count = taps.shape[0]
    chips = grid_x * grid_y
    result = (2, lanes, 2 * chips * lanes)
    dma = pltpu.SemaphoreType.DMA
    return pl.pallas_call(
        functools.partial(exchange_kernel, zs),
        out_shape=jax.ShapeDtypeStruct((1,) + result, jnp.float32),
        in_specs=[pl.BlockSpec(memory_space=pltpu.VMEM)] * 2,
        out_specs=pl.BlockSpec(memory_space=pltpu.VMEM),
        scratch_shapes=[
            pltpu.VMEM((zs, 2, 2, grid_y, grid_x, span, lanes), jnp.bfloat16),
            pltpu.VMEM((2 * lanes, 8 * span), jnp.bfloat16),
            pltpu.VMEM((2 * lanes, 4 * span), jnp.bfloat16),
            pltpu.VMEM((tap_count - 1 + span, 2 * zs, lanes), jnp.bfloat16),
            pltpu.VMEM(((2 * zs + 1) * span, lanes), jnp.float32),
            pltpu.VMEM((zs, 2, span, lanes), jnp.bfloat16),
            pltpu.VMEM((2, tap_count - 1, zs, lanes), volts.dtype),
            dma((2,)),
        ]
        + [dma((zs,))] * 7
        + [dma]
        + [dma((zs,))] * 3,
        compiler_params=pltpu.CompilerParams(
            collective_id=0, has_side_effects=True, vmem_limit_bytes=40 * 1024 * 1024
        ),
    )(volts, taps)


def body(voltages, fir_taps):
    norm_factor = 1.0 / (voltages.shape[1] * lax.axis_size("chan"))
    return exchange(voltages, fir_taps) * norm_factor


def solution(mesh):
    placed = (P(None, "chan", None, "inp"), P())
    return jax.shard_map(
        body, mesh=mesh, in_specs=placed, out_specs=P("chan", None, "inp", None), check_vma=False
    )
```

```python
import functools
import math

import jax
import jax.numpy as jnp
from jax import lax
from jax.experimental import pallas as pl
from jax.experimental.pallas import tpu as pltpu
from jax.sharding import PartitionSpec as P


volt_scale = 1.0 / 256.0
LAGS = (2, 4, 6, 6, 9, 13)
grid_x = 4
grid_y = 4
MESH = pl.DeviceIdType.MESH


def dft_entries(count, tap_count):
    shape = (2 * count, 2 * count * tap_count)
    row = lax.broadcasted_iota(jnp.int32, shape, 0)
    column = lax.broadcasted_iota(jnp.int32, shape, 1)
    channel, imag_out = row // 2, row % 2
    imag_in, sample = (column // count) % 2, column % count
    phase = (channel * sample + (imag_out - imag_in + 4) * (count // 4)) % count
    entries = jnp.zeros(shape, jnp.float32)
    for step in range(count):
        entries = jnp.where(phase == step, math.cos(2.0 * math.pi * step / count), entries)
    return entries


def exchange_kernel(
    zs, volts, taps, out,
    store, rows, last_rows, frames, stage_f32, spectra, rim, sem_rim,
    sem_a, sem_b, sem_c, sem_d, sem_f, sem_g, sem_p, send_a, send_b, send_r, send_p,
):
    chips = grid_x * grid_y
    span = spectra.shape[2]
    lanes = spectra.shape[3]
    reach = taps.shape[0]
    early = reach - 1
    z = lax.axis_index("chan")
    inp = lax.axis_index("inp")
    core = lax.rem(inp, 2)
    chip = lax.div(inp, 2)
    y = lax.rem(chip, grid_y)
    x = lax.div(chip, grid_y)
    here = ((x, y), (y, x))

    def wrap(index):
        return lax.rem(index + 4, 4)

    def device_of(part, u, v):
        first, second = (u, v) if part == 0 else (v, u)
        return (wrap(first) * grid_y + wrap(second)) * 2 + core

    partner = chip * 2 + 1 - core

    barrier = pltpu.get_barrier_semaphore()

    def greet_z(step, carry):
        pl.semaphore_signal(
            barrier, inc=1, device_id={"chan": lax.rem(z + step, zs)}, device_id_type=MESH
        )
        return carry

    lax.fori_loop(1, zs, greet_z, 0)
    for du, dv in ((1, 0), (-1, 0), (0, 1), (0, -1)):
        pl.semaphore_signal(
            barrier, inc=1, device_id={"inp": device_of(0, x + du, y + dv)}, device_id_type=MESH
        )
    pl.semaphore_signal(barrier, inc=1, device_id={"inp": partner}, device_id_type=MESH)

    for part in (0, 1):
        frames[early:, part * zs : (part + 1) * zs] = (
            volts[part].astype(jnp.float32).astype(jnp.bfloat16)
        )
    later_first = [taps[k : k + 1] for k in range(early, -1, -1) for part in (0, 1)]
    weights = dft_entries(zs, reach) * jnp.concatenate(later_first, 1)
    coarse = weights.astype(jnp.bfloat16)
    rest = weights - coarse.astype(jnp.float32)
    middle = rest.astype(jnp.bfloat16)
    fine = (rest - middle.astype(jnp.float32)).astype(jnp.bfloat16)
    pieces = jnp.concatenate([coarse, middle, fine], 0)
    outs = 2 * zs

    def channelize(*spots):
        columns = [frames[pl.ds(s, reach)].reshape(reach * outs, lanes) for s in spots]
        product = jnp.dot(pieces, jnp.concatenate(columns, 1), preferred_element_type=jnp.float32)
        total = (product[:outs] + (product[outs : 2 * outs] + product[2 * outs :])) * volt_scale
        for n, s in enumerate(spots):
            stage_f32[pl.ds(s, outs, stride=span), :] = total[:, n * lanes : (n + 1) * lanes]

    def channelize_pair(step, carry):
        channelize(early + step, early + step + half)
        return carry

    half = (span - early) // 2
    lax.fori_loop(0, half // 2, channelize_pair, 0, unroll=5)
    pl.semaphore_wait(barrier, zs + 4)

    rim_copy = pltpu.make_async_remote_copy(
        src_ref=volts.at[:, pl.ds(span - early, early)], dst_ref=rim,
        send_sem=sem_rim.at[0], recv_sem=sem_rim.at[1],
        device_id={"chan": lax.rem(z + 1, zs)}, device_id_type=MESH,
    )
    rim_copy.start()
    lax.fori_loop(half // 2, half, channelize_pair, 0, unroll=5)
    if early + 2 * half < span:
        channelize(span - 1)
    lead = min(16, span // 2)
    staged = stage_f32[: outs * span].reshape(spectra.shape)
    spectra[:, :, lead:] = staged[:, :, lead:].astype(jnp.bfloat16)
    out[...] = jnp.zeros_like(out)
    rim_copy.wait()
    for part in (0, 1):
        before = rim[part] * jnp.minimum(z, 1)
        frames[0:early, part * zs : (part + 1) * zs] = before.astype(jnp.float32).astype(jnp.bfloat16)
    for first in range(0, early, 2):
        channelize(*range(first, min(first + 2, early)))
    staged = stage_f32[: outs * span].reshape(spectra.shape)
    spectra[:, :, :lead] = staged[:, :, :lead].astype(jnp.bfloat16)

    def own_block(source, part):
        u, v = here[part]
        return store.at[source, core, part, v, u]

    for part in (0, 1):
        pltpu.make_async_copy(spectra.at[z, part], own_block(z, part), sem_a.at[z]).start()

    def offset_of(turn):
        return lax.div(turn + 1, 2) * (2 * lax.rem(turn, 2) - 1)

    def corner_turn(turn, carry):
        target = lax.rem(z + offset_of(turn) + zs, zs)
        for part in (0, 1):
            pltpu.make_async_remote_copy(
                src_ref=spectra.at[target, part], dst_ref=own_block(z, part),
                send_sem=send_a, recv_sem=sem_a.at[z],
                device_id={"chan": target}, device_id_type=MESH,
            ).start()
        return carry

    lax.fori_loop(1, zs, corner_turn, 0)

    def source_of(turn):
        return lax.rem(z + offset_of(turn) + zs, zs)

    def arrive(sem, ref):
        pltpu.make_async_copy(ref, ref, sem).wait()

    def give(ref, target, send, recv):
        pltpu.make_async_remote_copy(
            src_ref=ref, dst_ref=ref, send_sem=send, recv_sem=recv,
            device_id={"inp": target}, device_id_type=MESH,
        ).start()

    def stage(t, action):
        @pl.when(jnp.logical_and(t >= 0, t < zs))
        def _():
            action(t, source_of(t))

    def way_of(t, part):
        return 1 - 2 * lax.rem(t + part, 2)

    def give_block(t, k, part, shift):
        u, v = here[part]
        give(
            store.at[k, core, part, v, wrap(u + shift)], device_of(part, u, v + way_of(t, part)),
            send_r.at[t], sem_d.at[t],
        )

    def step_a(t, k):
        arrive(sem_a.at[k], store.at[k, core, :, 0, 0])
        for part in (0, 1):
            u, v = here[part]
            for side in (1, -1):
                give(store.at[k, core, part, v, u], device_of(part, u + side, v), send_b.at[t], sem_b.at[t])
        for part in (0, 1):
            give_block(t, k, part, 0)

    def step_b(t, k):
        arrive(sem_b.at[t], store.at[k, core, :, 0, pl.ds(0, 2)])
        for part in (0, 1):
            u, v = here[part]
            way = way_of(t, part)
            give(
                store.at[k, core, part, v, wrap(u - way)], device_of(part, u + way, v),
                send_b.at[t], sem_c.at[t],
            )
        for shift in (1, -1):
            for part in (0, 1):
                give_block(t, k, part, shift)

    def give_row(t, k, part, row, way, recv):
        u, v = here[part]
        give(store.at[k, core, part, wrap(row)], device_of(part, u, v + way), send_r.at[t], recv)

    def share_row(t, k, part, row):
        give(store.at[k, core, part, wrap(row)], partner, send_p.at[t], sem_p.at[t])

    def step_c(t, k):
        arrive(sem_c.at[t], store.at[k, core, :, 0, 0])
        for part in (0, 1):
            give_block(t, k, part, 2)

    def step_f(t, k):
        for part in (0, 1):
            give_row(t, k, part, here[part][1], -way_of(t, part), sem_f.at[t])

    def step_d(t, k):
        arrive(sem_d.at[t], store.at[k, core, :, 0])
        for part in (0, 1):
            v = here[part][1]
            way = way_of(t, part)
            give_row(t, k, part, v - way, way, sem_g.at[t])
        for part in (0, 1):
            v = here[part][1]
            share_row(t, k, part, v)
            share_row(t, k, part, v - way_of(t, part))

    def step_e(t, k):
        arrive(sem_f.at[t], store.at[k, core, :, 0])
        arrive(sem_g.at[t], store.at[k, core, :, 0])
        for part in (0, 1):
            v = here[part][1]
            share_row(t, k, part, v + way_of(t, part))
            share_row(t, k, part, v + 2)

    def correlate(t, count, quarter, rows):
        ks = [source_of(t + step) for step in range(count)]

        @pl.when(quarter == 0)
        def _():
            for step, k in enumerate(ks):
                arrive(sem_p.at[t + step], store.at[k, 1 - core])
            depth = count * span
            mine = []
            for part in (0, 1):
                u, v = here[part]
                both = jnp.concatenate([store[k, core, part, v, u] for k in ks], 0)
                mine.append(both.astype(jnp.float32).T)
            real, imag = mine
            rows[:lanes, :depth] = real.astype(jnp.bfloat16)
            rows[:lanes, depth:] = imag.astype(jnp.bfloat16)
            rows[lanes:, :depth] = imag.astype(jnp.bfloat16)
            rows[lanes:, depth:] = (-real).astype(jnp.bfloat16)

        left = rows[...]
        for second in range(grid_y):
            block = jnp.concatenate(
                [
                    jnp.concatenate([store[k, c, 0, second, quarter] for c in (0, 1)], 1) for k in ks
                ]
                + [
                    jnp.concatenate([store[k, c, 1, quarter, second] for c in (0, 1)], 1) for k in ks
                ],
                0,
            )
            product = jnp.dot(left, block, preferred_element_type=jnp.float32)
            begin = (quarter * grid_y + second) * (2 * lanes)
            columns = pl.ds(pl.multiple_of(begin, 2 * lanes), 2 * lanes)
            out[0, 0, :, columns] += product[:lanes]
            out[0, 1, :, columns] += product[lanes:]

    def settle(t, k):
        arrive(send_b.at[t], store.at[0, 0, :, 0, pl.ds(0, 3)])
        arrive(send_r.at[t], store.at[0, 0, :, pl.ds(0, 3)])
        arrive(send_p.at[t], store.at[0, 0])

    def finish(t):
        def one_quarter(quarter, carry):
            correlate(t, 2, quarter, last_rows)
            return carry

        return one_quarter

    def iteration(it, carry):
        stage(it, step_a)
        stage(it - LAGS[0], step_b)
        stage(it - LAGS[1], step_c)
        stage(it - LAGS[3], step_f)
        late = it - LAGS[5]

        @pl.when(jnp.logical_and(late >= 0, late < zs - 4))
        def _():
            quarter = lax.rem(late, 4)
            correlate(late - quarter, 4, quarter, rows)

        ending = it - (zs + LAGS[4] - 2)

        @pl.when(ending >= 0)
        def _():
            lax.fori_loop(2 * ending, 2 * ending + 2, finish(zs - 4), 0)

        stage(it - LAGS[2], step_d)
        stage(it - LAGS[4], step_e)
        stage(it - LAGS[4] - 2, settle)
        return carry

    lax.fori_loop(0, zs + LAGS[4], iteration, 0)
    arrive(send_a, spectra.at[pl.ds(0, zs - 1)])
    lax.fori_loop(0, 4, finish(zs - 2), 0)
    for t in (zs - 2, zs - 1):
        settle(t, 0)


def exchange(volts, taps):
    parts, span, zs, lanes = volts.shape
    tap_count = taps.shape[0]
    chips = grid_x * grid_y
    result = (2, lanes, 2 * chips * lanes)
    dma = pltpu.SemaphoreType.DMA
    return pl.pallas_call(
        functools.partial(exchange_kernel, zs),
        out_shape=jax.ShapeDtypeStruct((1,) + result, jnp.float32),
        in_specs=[pl.BlockSpec(memory_space=pltpu.VMEM)] * 2,
        out_specs=pl.BlockSpec(memory_space=pltpu.VMEM),
        scratch_shapes=[
            pltpu.VMEM((zs, 2, 2, grid_y, grid_x, span, lanes), jnp.bfloat16),
            pltpu.VMEM((2 * lanes, 8 * span), jnp.bfloat16),
            pltpu.VMEM((2 * lanes, 4 * span), jnp.bfloat16),
            pltpu.VMEM((tap_count - 1 + span, 2 * zs, lanes), jnp.bfloat16),
            pltpu.VMEM(((2 * zs + 1) * span, lanes), jnp.float32),
            pltpu.VMEM((zs, 2, span, lanes), jnp.bfloat16),
            pltpu.VMEM((2, tap_count - 1, zs, lanes), volts.dtype),
            dma((2,)),
        ]
        + [dma((zs,))] * 7
        + [dma]
        + [dma((zs,))] * 3,
        compiler_params=pltpu.CompilerParams(
            collective_id=0, has_side_effects=True, vmem_limit_bytes=40 * 1024 * 1024
        ),
    )(volts, taps)


def body(voltages, fir_taps):
    norm_factor = 1.0 / (voltages.shape[1] * lax.axis_size("chan"))
    return exchange(voltages, fir_taps) * norm_factor


def solution(mesh):
    placed = (P(None, "chan", None, "inp"), P())
    return jax.shard_map(
        body, mesh=mesh, in_specs=placed, out_specs=P("chan", None, "inp", None), check_vma=False
    )
```
